32 devices in a mesh: row: 8 (over y, x, core), col: 4 (over z).
Axes of the slice: x: 2, y: 2, z: 4, core: 2. Of those that a mesh axis runs over, the one named last changes fastest.
Arguments:
- object_field: float32 [2, 4096, 2048], P(None, 'row', 'col'), may hold values from -6 to 6
- probe: float32 [2, 4, 256, 256], replicated, may hold values from -5 to 5
- amplitudes: float32 [8, 4, 6, 256, 256], P('row', 'col'), may hold values from 0.1 to 2
- positions: int32 [8, 4, 6, 2], P('row', 'col'), may hold values from 1 to 511, as said below
- counts: int32 [8, 4], P('row', 'col'), may hold values from 1 to 6, as said below
Outputs:
- object_new: float32 [2, 4096, 2048], P(None, 'row', 'col')
- probe_new: float32 [2, 4, 256, 256], replicated
- position_grad: float32 [8, 4, 6, 2], P('row', 'col')
The draws below stay inside these ranges and needn't reach their ends.
Inputs may be any that keep to these rules, and one draw needn't show every extreme that they name: `counts`: live scan positions of each tile; slots at or past the count are unused and ignored; some tile has all 6 slots live. `positions`: offset of a patch's first cell in its tile extended by 128 cells on each side.
All inputs are finite; a program needn't handle non-finite values.
Results may differ from the reference program's by a relative error of at most 0.0003.
Values sent between devices are 32-bit elements; how exact they have to be, the bound alone decides.
No kernel may reach another device: no remote copies, remote signals or barrier semaphores. Data moves between devices by JAX's collectives and lax.ppermute only.
A program may use at most 192 MiB of HBM per device.

```python
import jax
import jax.numpy as jnp
from jax import lax

P_SIZE = 256
MODES = 4
HALO = 128
TILE = 512
POS_CAP = 6
NR = 4096
NC = 2048
N_ROW = 8
N_COL = 4


def draw_positions(key, part):
    upper = TILE + 2 * HALO - P_SIZE
    values = jax.random.randint(key, (N_ROW, N_COL, POS_CAP, 2), 1, upper)
    values = values.at[0, 0, 0, 0].set(1)
    values = values.at[0, 0, 0, 1].set(upper - 1)
    return values.astype(jnp.int32)


def draw_counts(key, part):
    total_tiles = N_ROW * N_COL
    low_key, pick_key = jax.random.split(key, 2)
    values = jax.random.randint(low_key, (total_tiles,), max(POS_CAP // 2, 1), POS_CAP + 1)
    chosen = jax.random.randint(pick_key, (), 0, total_tiles)
    values = values.at[chosen].set(POS_CAP)
    values = values.at[(chosen + 1) % total_tiles].set(1)
    return values.reshape(N_ROW, N_COL).astype(jnp.int32)


def shard_levels(rng, extent, cuts, smallest, high):
    level = 1.0
    for axis_at, blocks in cuts:
        steps = jax.random.uniform(jax.random.fold_in(jax.random.fold_in(rng, 6), axis_at), (blocks,), jnp.float32, smallest / len(cuts), high / len(cuts))
        level = level * jnp.repeat(jnp.exp(steps), extent[axis_at] // blocks).reshape((-1,) + (1,) * (len(extent) - 1 - axis_at))
    return level


def bell_draw(key, dims, width, most, cuts=(), kind=jnp.bfloat16):
    drawn = width * jax.random.normal(key, dims, jnp.float32)
    if cuts:
        drawn = drawn * shard_levels(key, dims, cuts, -0.22, 0.18)
    return jnp.clip(drawn, -most, most).astype(kind)


def setup_inputs(seed: int = 0) -> dict:
    arg_keys = jax.random.split(jax.random.key(seed), 6)
    object_field = bell_draw(arg_keys[0], (2, NR, NC), 1.0, 6.0, ((1, 8), (2, 4)), jnp.float32)
    probe = bell_draw(arg_keys[1], (2, MODES, P_SIZE, P_SIZE), 0.35, 5.0, (), jnp.float32)
    amplitudes = jnp.clip(0.1 + 1.9 * jax.random.uniform(arg_keys[2], (N_ROW, N_COL, POS_CAP, P_SIZE, P_SIZE), jnp.float32) ** shard_levels(arg_keys[2], (N_ROW, N_COL, POS_CAP, P_SIZE, P_SIZE), ((0, 8), (1, 4)), -0.2, 0.2), 0.1, 2.0)
    positions = draw_positions(jax.random.fold_in(arg_keys[5], 71), 0)
    counts = draw_counts(jax.random.fold_in(arg_keys[5], 71), 0)
    return {"object_field": object_field, "probe": probe, "amplitudes": amplitudes, "positions": positions, "counts": counts}


INTENSITY_FLOOR = 0.1
EPSILON = 1e-06

def reference(object_field, probe, amplitudes, positions, counts):
    padded = jnp.pad(object_field, ((0, 0), (HALO, HALO), (HALO, HALO)))
    probe_c = lax.complex(probe[0], probe[1])
    total_items = N_ROW * N_COL * POS_CAP
    items = jnp.arange(total_items, dtype=jnp.int32)
    tile_row = items // (N_COL * POS_CAP)
    tile_col = items // POS_CAP % N_COL
    slot_index = items % POS_CAP
    flat_pos = positions.reshape(total_items, 2).astype(jnp.int32)
    live_all = (slot_index < counts.reshape(-1)[tile_row * N_COL + tile_col]).astype(object_field.dtype)
    flat_amp = amplitudes.reshape(total_items, P_SIZE, P_SIZE)

    def visit_item(carry, item):
        spread, probe_grad, energy = carry
        row_start = (tile_row[item] * TILE + flat_pos[item, 0]).astype(jnp.int32)
        col_start = (tile_col[item] * TILE + flat_pos[item, 1]).astype(jnp.int32)
        window = lax.dynamic_slice(padded, (jnp.int32(0), row_start - 1, col_start - 1), (2, P_SIZE + 2, P_SIZE + 2))
        live_flag = live_all[item]
        patch_c = lax.complex(window[0, 1:-1, 1:-1], window[1, 1:-1, 1:-1])
        exit_wave = probe_c * patch_c[None]
        far_field = jnp.fft.fft2(exit_wave, norm='ortho')
        intensity = lax.optimization_barrier(jnp.sum(jnp.real(far_field) ** 2 + jnp.imag(far_field) ** 2, axis=0))
        modulus = flat_amp[item] / jnp.sqrt(jnp.maximum(intensity, INTENSITY_FLOOR))
        correction = jnp.fft.ifft2(far_field * modulus[None], norm='ortho') - exit_wave
        gradient = lax.optimization_barrier(jnp.sum(jnp.conj(probe_c) * correction, axis=0)) * live_flag
        grad_pair = jnp.stack([jnp.real(gradient), jnp.imag(gradient)])
        probe_term = jnp.conj(patch_c)[None] * correction * live_flag
        probe_grad = probe_grad + jnp.stack([jnp.real(probe_term), jnp.imag(probe_term)])
        energy = energy + live_flag * jnp.mean(jnp.real(patch_c) ** 2 + jnp.imag(patch_c) ** 2)
        corner_at = (jnp.int32(0), row_start, col_start)
        current = lax.dynamic_slice(spread, corner_at, (2, P_SIZE, P_SIZE))
        spread = lax.dynamic_update_slice(spread, current + grad_pair, corner_at)
        slope_rows = 0.5 * (window[:, 2:, 1:-1] - window[:, :-2, 1:-1])
        slope_cols = 0.5 * (window[:, 1:-1, 2:] - window[:, 1:-1, :-2])
        shift_grad = jnp.stack([jnp.sum(grad_pair * slope_rows) / P_SIZE, jnp.sum(grad_pair * slope_cols) / P_SIZE])
        return ((spread, probe_grad, energy), shift_grad)
    start_carry = (jnp.zeros(padded.shape, object_field.dtype), jnp.zeros_like(probe), jnp.zeros((), object_field.dtype))
    (spread, probe_grad, energy), shift_all = lax.scan(visit_item, start_carry, items)
    fold = spread[:, HALO:HALO + object_field.shape[1], HALO:HALO + object_field.shape[2]]
    illumination = jnp.max(lax.optimization_barrier(jnp.sum(probe * probe, axis=(0, 1))))
    object_new = object_field + fold / illumination
    probe_new = probe + probe_grad / (energy + EPSILON)
    position_grad = shift_all.reshape(N_ROW, N_COL, POS_CAP, 2)
    return (object_new, probe_new, position_grad)
```

```python
import functools
import math

import jax
import jax.numpy as jnp
from jax import lax
from jax.experimental import pallas as pl
from jax.experimental.pallas import tpu as pltpu
from jax.sharding import PartitionSpec as P

HALO = 128
INTENSITY_FLOOR = 0.1
EPSILON = 1e-06
F32 = jnp.float32
BF16 = jnp.bfloat16
LANE = 128
SUB = 8
CHUNKS = ((0, 1, 2, 3),)


def split_table(w):
    hi = lax.reduce_precision(w, 8, 7)
    return hi.astype(BF16), (w - hi).astype(BF16)


def tables(pixels):
    half = pixels // 2
    n = jnp.arange(half, dtype=jnp.int32)
    out = []
    for parity in (0, 1):
        turns = (n[:, None] * (2 * n[None, :] + parity)) % pixels
        angle = turns.astype(F32) * (2.0 * math.pi / pixels)
        c = jnp.cos(angle) * (1.0 / math.sqrt(pixels))
        s = jnp.sin(angle) * (1.0 / math.sqrt(pixels))
        w = jnp.concatenate(
            [jnp.concatenate([c, -s], axis=1), jnp.concatenate([s, c], axis=1)], axis=0
        )
        hi, lo = split_table(w)
        thi, tlo = hi.T, lo.T
        out.append(
            (
                jnp.concatenate([hi, hi, lo], axis=0),
                jnp.concatenate([thi, thi, tlo], axis=1),
                jnp.concatenate([thi, thi, tlo], axis=0),
                jnp.concatenate([hi, hi, lo], axis=1),
            )
        )
    (fre, fle, ire, ile), (fro, flo, iro, ilo) = out
    return (fre, fro, fle, flo), (ire, iro, ile, ilo)


def parity_matrix(pixels):
    half = pixels // 2
    x = lax.broadcasted_iota(jnp.int32, (pixels, pixels), 0)
    j = lax.broadcasted_iota(jnp.int32, (pixels, pixels), 1)
    target = jnp.where(j < half, 2 * j, 2 * (j - half) + 1)
    one = (x == target).astype(BF16)
    return jnp.concatenate([one, one, one], axis=0)


def halves(x):
    hi = x.astype(BF16)
    lo = (x - hi.astype(F32)).astype(BF16)
    return hi, lo


def matmul(a, b):
    return jnp.dot(a, b, preferred_element_type=F32)


def from_left(table, x):
    hi, lo = halves(x)
    return matmul(table, jnp.concatenate([hi, lo, hi], axis=0))


def from_right(x, table):
    hi, lo = halves(x)
    return matmul(jnp.concatenate([hi, lo, hi], axis=1), table)


def fold_block(x):
    rows, cols = x.shape
    y = jnp.sum(x.reshape(rows // SUB, SUB, cols), axis=0)
    z = y[:, :LANE]
    for c in range(LANE, cols, LANE):
        z = z + y[:, c : c + LANE]
    return z


def forward_kernel(
    pos_ref, cnt_ref, *refs, modes, pixels, tile, grid_shape, chunks
):
    n_pieces = len(grid_shape)
    pieces = refs[:n_pieces]
    probe_ref, amp_left, amp_right, fre, fro, fle, flo, perm = refs[n_pieces : n_pieces + 8]
    patch_ref, energy_ref = refs[n_pieces + 8 : n_pieces + 10]
    g_refs = refs[n_pieces + 10 : n_pieces + 10 + len(chunks)]
    ext, far, sem = refs[n_pieces + 10 + len(chunks) :]
    s = pl.program_id(0)
    half = pixels // 2

    @pl.when(s == 0)
    def _():
        copies = []
        for i, (r0, c0, rn, cn) in enumerate(grid_shape):
            copies.append(
                pltpu.make_async_copy(
                    pieces[i], ext.at[:, pl.ds(r0, rn), pl.ds(c0, cn)], sem.at[i]
                )
            )
        for c in copies:
            c.start()
        energy_ref[...] = jnp.zeros_like(energy_ref)
        for c in copies:
            c.wait()

    @pl.when(s < cnt_ref[0])
    def _():
        a = pos_ref[s, 0]
        b = pos_ref[s, 1]
        qa, qb = a // SUB, b // LANE
        ta, tb = a - qa * SUB, b - qb * LANE
        rows, cols = pixels + SUB, pixels + LANE
        r0 = pl.multiple_of(qa * SUB, SUB)
        c0 = pl.multiple_of(qb * LANE, LANE)
        parts = []
        for part in range(2):
            blk = ext[part, pl.ds(r0, rows), pl.ds(c0, cols)]
            blk = pltpu.roll(blk, lax.rem(cols - tb, cols), 1)[:, :pixels]
            blk = pltpu.roll(blk, lax.rem(rows - ta, rows), 0)[:pixels]
            parts.append(blk)
            patch_ref[0, part] = blk
        energy_ref[...] += fold_block(parts[0] * parts[0] + parts[1] * parts[1])

        total_e = None
        for k in range(modes):
            o_r, o_i = patch_ref[0, 0], patch_ref[0, 1]
            p_r, p_i = probe_ref[0, k], probe_ref[1, k]
            w_r = p_r * o_r - p_i * o_i
            w_i = p_r * o_i + p_i * o_r
            even = jnp.concatenate(
                [w_r[:half] + w_r[half:], w_i[:half] + w_i[half:]], axis=0
            )
            odd = jnp.concatenate(
                [w_r[:half] - w_r[half:], w_i[:half] - w_i[half:]], axis=0
            )
            ue = from_left(fle[...], even)
            uo = from_left(flo[...], odd)
            u_r = jnp.concatenate([ue[:half], uo[:half]], axis=0)
            u_i = jnp.concatenate([ue[half:], uo[half:]], axis=0)
            be = jnp.concatenate(
                [u_r[:, :half] + u_r[:, half:], u_i[:, :half] + u_i[:, half:]], axis=1
            )
            bo = jnp.concatenate(
                [u_r[:, :half] - u_r[:, half:], u_i[:, :half] - u_i[:, half:]], axis=1
            )
            far[k, 0] = from_right(be, fre[...])
            far[k, 1] = from_right(bo, fro[...])

        amp = jnp.concatenate(
            [
                jnp.concatenate([ref[0, pl.ds(p, half, stride=2), :] for p in range(2)], axis=0)
                for ref in (amp_left, amp_right)
            ],
            axis=1,
        )
        a_hi = amp.astype(BF16)
        a_rest = amp - a_hi.astype(F32)
        a_mid, a_lo = halves(a_rest)
        amp = matmul(jnp.concatenate([a_hi, a_mid, a_lo], axis=1), perm[...])
        for p in range(2):
            inten = None
            for k in range(modes):
                f = far[k, p]
                t = f * f
                t = t[:, :half] + t[:, half:]
                inten = t if inten is None else inten + t
            mod = amp[:, p * half : (p + 1) * half] * lax.rsqrt(
                jnp.maximum(inten, INTENSITY_FLOOR)
            )
            mod = jnp.concatenate([mod, mod], axis=1)
            for c, group in enumerate(chunks):
                for i, k in enumerate(group):
                    hi, lo = halves(far[k, p] * mod)
                    g_refs[c][0, i, p, 0] = hi
                    g_refs[c][0, i, p, 1] = lo


def backward_kernel(cnt_ref, *refs, modes, pixels, first):
    if first:
        g_ref, patch_ref, probe_ref, ire, iro, ile, ilo, grad_ref, pgrad_ref = refs
        prev_ref = None
    else:
        g_ref, patch_ref, probe_ref, ire, iro, ile, ilo, prev_ref, grad_ref, pgrad_ref = refs
    s = pl.program_id(0)
    half = pixels // 2
    live = s < cnt_ref[0]

    @pl.when(s == 0)
    def _():
        pgrad_ref[...] = jnp.zeros_like(pgrad_ref)

    @pl.when(jnp.logical_not(live))
    def _():
        grad_ref[...] = jnp.zeros_like(grad_ref)

    @pl.when(live)
    def _():
        for i in range(modes):
            e_hi, e_lo = g_ref[0, i, 0, 0], g_ref[0, i, 0, 1]
            o_hi, o_lo = g_ref[0, i, 1, 0], g_ref[0, i, 1, 1]
            e = matmul(jnp.concatenate([e_hi, e_lo, e_hi], axis=1), ire[...])
            o = matmul(jnp.concatenate([o_hi, o_lo, o_hi], axis=1), iro[...])
            x0, x1 = e + o, e - o
            ke = jnp.concatenate(
                [
                    jnp.concatenate([x0[:half, :half], x1[:half, :half]], axis=1),
                    jnp.concatenate([x0[:half, half:], x1[:half, half:]], axis=1),
                ],
                axis=0,
            )
            ko = jnp.concatenate(
                [
                    jnp.concatenate([x0[half:, :half], x1[half:, :half]], axis=1),
                    jnp.concatenate([x0[half:, half:], x1[half:, half:]], axis=1),
                ],
                axis=0,
            )
            ev = from_left(ile[...], ke)
            od = from_left(ilo[...], ko)
            for h in range(2):
                rs = pl.ds(h * half, half)
                back = ev + od if h == 0 else ev - od
                b_r, b_i = back[:half], back[half:]
                o_r, o_i = patch_ref[0, 0, rs, :], patch_ref[0, 1, rs, :]
                p_r, p_i = probe_ref[0, i, rs, :], probe_ref[1, i, rs, :]
                f_r = b_r - (p_r * o_r - p_i * o_i)
                f_i = b_i - (p_r * o_i + p_i * o_r)
                g_r = p_r * f_r + p_i * f_i
                g_i = p_r * f_i - p_i * f_r
                if i == 0 and first:
                    grad_ref[0, 0, rs, :] = g_r
                    grad_ref[0, 1, rs, :] = g_i
                elif i == 0:
                    grad_ref[0, 0, rs, :] = prev_ref[0, 0, rs, :] + g_r
                    grad_ref[0, 1, rs, :] = prev_ref[0, 1, rs, :] + g_i
                else:
                    grad_ref[0, 0, rs, :] += g_r
                    grad_ref[0, 1, rs, :] += g_i
                pgrad_ref[0, i, rs, :] += o_r * f_r + o_i * f_i
                pgrad_ref[1, i, rs, :] += o_r * f_i - o_i * f_r


def place_kernel(pos_ref, cnt_ref, grad_ref, *refs, pixels, grid_shape):
    outs = refs[: len(grid_shape)]
    canvas, sem = refs[len(grid_shape) :]
    canvas[...] = jnp.zeros_like(canvas)
    rows, cols = pixels + SUB, pixels + LANE

    def step(s, carry):
        a = pos_ref[s, 0]
        b = pos_ref[s, 1]
        qa, qb = a // SUB, b // LANE
        ta, tb = a - qa * SUB, b - qb * LANE
        r0 = pl.multiple_of(qa * SUB, SUB)
        c0 = pl.multiple_of(qb * LANE, LANE)
        for part in range(2):
            g = grad_ref[s, part]
            g = jnp.concatenate([g, jnp.zeros((SUB, pixels), F32)], axis=0)
            g = pltpu.roll(g, ta, 0)
            g = jnp.concatenate([g, jnp.zeros((rows, LANE), F32)], axis=1)
            g = pltpu.roll(g, tb, 1)
            canvas[part, pl.ds(r0, rows), pl.ds(c0, cols)] += g
        return carry

    lax.fori_loop(0, cnt_ref[0], step, 0)
    copies = []
    for i, (r0, c0, rn, cn) in enumerate(grid_shape):
        copies.append(
            pltpu.make_async_copy(
                canvas.at[:, pl.ds(r0, rn), pl.ds(c0, cn)], outs[i], sem.at[i]
            )
        )
    for c in copies:
        c.start()
    for c in copies:
        c.wait()


def slope_kernel(pos_ref, cnt_ref, grad_ref, *refs, pixels, grid_shape, extent):
    pieces = refs[: len(grid_shape)]
    out_ref, ext, sem = refs[len(grid_shape) :]
    s = pl.program_id(0)
    out_ref[...] = jnp.zeros_like(out_ref)

    @pl.when(s == 0)
    def _():
        copies = []
        for i, (r0, c0, rn, cn) in enumerate(grid_shape):
            copies.append(
                pltpu.make_async_copy(
                    pieces[i], ext.at[:, pl.ds(r0, rn), pl.ds(c0, cn)], sem.at[i]
                )
            )
        for c in copies:
            c.start()
        for c in copies:
            c.wait()

    @pl.when(s < cnt_ref[0])
    def _():
        rows, cols = pixels + 2 * SUB, pixels + 2 * LANE
        a = pos_ref[s, 0]
        b = pos_ref[s, 1]
        qa = jnp.minimum((a - 1) // SUB, (extent - rows) // SUB)
        qb = jnp.minimum((b - 1) // LANE, (extent - cols) // LANE)
        ta, tb = a - qa * SUB, b - qb * LANE
        r0 = pl.multiple_of(qa * SUB, SUB)
        c0 = pl.multiple_of(qb * LANE, LANE)
        acc_r = jnp.zeros((SUB, LANE), F32)
        acc_c = jnp.zeros((SUB, LANE), F32)
        for part in range(2):
            w = ext[part, pl.ds(r0, rows), pl.ds(c0, cols)]
            w = pltpu.roll(w, lax.rem(cols + LANE - tb, cols), 1)
            w = pltpu.roll(w, lax.rem(rows + SUB - ta, rows), 0)
            g = grad_ref[0, part]
            mid = w[:, LANE : LANE + pixels]
            down = pltpu.roll(mid, rows - 1, 0)[SUB : SUB + pixels]
            up = pltpu.roll(mid, 1, 0)[SUB : SUB + pixels]
            acc_r = acc_r + fold_block(g * (down - up))
            band = w[SUB : SUB + pixels]
            right = pltpu.roll(band, cols - 1, 1)[:, LANE : LANE + pixels]
            left = pltpu.roll(band, 1, 1)[:, LANE : LANE + pixels]
            acc_c = acc_c + fold_block(g * (right - left))
        out_ref[0, 0] = acc_r
        out_ref[0, 1] = acc_c


def neighbour(x, axis, by):
    peers = lax.axis_size(axis)
    pairs = [(i, i + by) for i in range(peers) if 0 <= i + by < peers]
    return lax.ppermute(x, axis, pairs)


def neighbour2(x, by_row, by_col):
    rows, cols = lax.axis_size("row"), lax.axis_size("col")
    pairs = [
        (i * cols + j, (i + by_row) * cols + j + by_col)
        for i in range(rows)
        for j in range(cols)
        if 0 <= i + by_row < rows and 0 <= j + by_col < cols
    ]
    return lax.ppermute(x, ("row", "col"), pairs)


def body(object_field, probe, amplitudes, positions, counts):
    tile = object_field.shape[1]
    modes, pixels = probe.shape[1], probe.shape[2]
    slots = positions.shape[2]
    extent = tile + 2 * HALO
    pos = positions[0, 0]
    cnt = counts[0]
    chunks = tuple(
        tuple(range(i, i + 4)) for i in range(0, modes, 4)
    ) if modes != 4 else CHUNKS

    lo, hi = HALO, HALO + tile
    where = {-1: (0, HALO), 0: (lo, tile), 1: (hi, HALO)}
    order = [(0, 0)] + [(i, j) for i in (-1, 0, 1) for j in (-1, 0, 1) if (i, j) != (0, 0)]
    shape_of = [
        (where[i][0], where[j][0], where[i][1], where[j][1]) for i, j in order
    ]

    def edge(i, n):
        return slice(None) if i == 0 else (slice(0, n) if i > 0 else slice(tile - n, tile))

    pieces = [object_field]
    for i, j in order[1:]:
        cut = object_field[:, edge(i, HALO), edge(j, HALO)]
        pieces.append(neighbour2(cut, -i, -j))

    fwd_tables, inv_tables = tables(pixels)
    perm = parity_matrix(pixels)
    illumination = jnp.max(jnp.sum(probe * probe, axis=(0, 1)))

    any_spec = pl.BlockSpec(memory_space=pl.ANY)

    def whole(x):
        nd = x.ndim
        return pl.BlockSpec(x.shape, lambda s, *_: (0,) * nd)

    patch_spec = pl.BlockSpec((1, 2, pixels, pixels), lambda s, *_: (s, 0, 0, 0))
    grad_shape = jax.ShapeDtypeStruct((slots, 2, pixels, pixels), F32)

    def g_spec(group):
        return pl.BlockSpec(
            (1, len(group), 2, 2, pixels, pixels), lambda s, *_: (s, 0, 0, 0, 0, 0)
        )

    outs = pl.pallas_call(
        functools.partial(
            forward_kernel,
            modes=modes,
            pixels=pixels,
            tile=tile,
            grid_shape=shape_of,
            chunks=chunks,
        ),
        grid_spec=pltpu.PrefetchScalarGridSpec(
            num_scalar_prefetch=2,
            grid=(slots,),
            in_specs=[any_spec] * len(pieces)
            + [whole(probe)]
            + [
                pl.BlockSpec((1, pixels, pixels // 2), lambda s, *_: (s, 0, 0)),
                pl.BlockSpec((1, pixels, pixels // 2), lambda s, *_: (s, 0, 1)),
            ]
            + [whole(t) for t in fwd_tables]
            + [whole(perm)],
            out_specs=[patch_spec, pl.BlockSpec((SUB, LANE), lambda s, *_: (0, 0))]
            + [g_spec(g) for g in chunks],
            scratch_shapes=[
                pltpu.VMEM((2, extent, extent), F32),
                pltpu.VMEM((modes, 2, pixels, pixels), F32),
                pltpu.SemaphoreType.DMA((len(pieces),)),
            ],
        ),
        out_shape=[grad_shape, jax.ShapeDtypeStruct((SUB, LANE), F32)]
        + [
            jax.ShapeDtypeStruct((slots, len(g), 2, 2, pixels, pixels), BF16) for g in chunks
        ],
        compiler_params=pltpu.CompilerParams(vmem_limit_bytes=56 << 20),
        name="forward",
    )(pos, cnt, *pieces, probe, amplitudes[0, 0], amplitudes[0, 0], *fwd_tables, perm)
    patches, energy_block = outs[0], outs[1]
    gs = outs[2:]
    energy = lax.psum(jnp.sum(energy_block) / (pixels * pixels), ("row", "col"))

    grad = None
    probe_parts = []
    devices = lax.axis_size("row") * lax.axis_size("col")
    me = lax.axis_index(("row", "col"))
    for group, g in zip(chunks, gs):
        n = len(group)
        part = probe[:, group[0] : group[0] + n] if n != modes else probe
        first = grad is None
        grad, pgrad = pl.pallas_call(
            functools.partial(backward_kernel, modes=n, pixels=pixels, first=first),
            grid_spec=pltpu.PrefetchScalarGridSpec(
                num_scalar_prefetch=1,
                grid=(slots,),
                in_specs=[g_spec(group), patch_spec, whole(part)]
                + [whole(t) for t in inv_tables]
                + ([] if first else [patch_spec]),
                out_specs=[
                    patch_spec,
                    pl.BlockSpec((2, n, pixels, pixels), lambda s, *_: (0, 0, 0, 0)),
                ],
            ),
            out_shape=[grad_shape, jax.ShapeDtypeStruct((2, n, pixels, pixels), F32)],
            compiler_params=pltpu.CompilerParams(vmem_limit_bytes=56 << 20),
            name="backward",
        )(cnt, g, patches, part, *inv_tables, *([] if first else [grad]))
        flat = pgrad.reshape(-1, pixels)
        share = lax.psum_scatter(flat, ("row", "col"), scatter_dimension=0, tiled=True)
        rows = flat.shape[0] // devices
        own = lax.dynamic_slice_in_dim(part.reshape(-1, pixels), me * rows, rows, 0)
        new = own + share / (energy + EPSILON)
        new = lax.all_gather(new, ("row", "col"), axis=0, tiled=True)
        probe_parts.append(new.reshape(2, n, pixels, pixels))
    probe_new = (
        probe_parts[0] if len(probe_parts) == 1 else jnp.concatenate(probe_parts, axis=1)
    )

    placed = pl.pallas_call(
        functools.partial(place_kernel, pixels=pixels, grid_shape=shape_of),
        grid_spec=pltpu.PrefetchScalarGridSpec(
            num_scalar_prefetch=2,
            grid=(1,),
            in_specs=[whole(grad)],
            out_specs=[any_spec] * len(order),
            scratch_shapes=[
                pltpu.VMEM((2, extent, extent), F32),
                pltpu.SemaphoreType.DMA((len(order),)),
            ],
        ),
        out_shape=[jax.ShapeDtypeStruct((2, rn, cn), F32) for _, _, rn, cn in shape_of],
        compiler_params=pltpu.CompilerParams(vmem_limit_bytes=56 << 20),
        name="place",
    )(pos, cnt, grad)
    arrived = [neighbour2(x, i, j) for (i, j), x in zip(order[1:], placed[1:])]

    slopes = pl.pallas_call(
        functools.partial(
            slope_kernel, pixels=pixels, grid_shape=shape_of, extent=extent
        ),
        grid_spec=pltpu.PrefetchScalarGridSpec(
            num_scalar_prefetch=2,
            grid=(slots,),
            in_specs=[patch_spec] + [any_spec] * len(pieces),
            out_specs=pl.BlockSpec((1, 2, SUB, LANE), lambda s, *_: (s, 0, 0, 0)),
            scratch_shapes=[
                pltpu.VMEM((2, extent, extent), F32),
                pltpu.SemaphoreType.DMA((len(pieces),)),
            ],
        ),
        out_shape=jax.ShapeDtypeStruct((slots, 2, SUB, LANE), F32),
        compiler_params=pltpu.CompilerParams(vmem_limit_bytes=56 << 20),
        name="slopes",
    )(pos, cnt, grad, *pieces)
    position_grad = (jnp.sum(slopes, axis=(2, 3)) * (0.5 / pixels))[None, None]

    fold = placed[0]
    for (i, j), x in zip(order[1:], arrived):
        gap = {0: (0, 0), 1: (0, tile - HALO), -1: (tile - HALO, 0)}
        fold = fold + jnp.pad(x, ((0, 0), gap[i], gap[j]))
    object_new = object_field + fold / illumination
    return (object_new, probe_new, position_grad)


def solution(mesh):
    return jax.shard_map(
        body,
        mesh=mesh,
        in_specs=(
            P(None, "row", "col"),
            P(),
            P("row", "col", None, None, None),
            P("row", "col", None, None),
            P("row", "col"),
        ),
        out_specs=(P(None, "row", "col"), P(), P("row", "col", None, None)),
        check_vma=False,
    )
```

```python
import functools
import math

import jax
import jax.numpy as jnp
from jax import lax
from jax.experimental import pallas as pl
from jax.experimental.pallas import tpu as pltpu
from jax.sharding import PartitionSpec as P

HALO = 128
INTENSITY_FLOOR = 0.1
EPSILON = 1e-06
F32 = jnp.float32
BF16 = jnp.bfloat16
LANE = 128
SUB = 8
CHUNKS = ((0, 1, 2, 3),)


def halves(x):
    hi = x.astype(BF16)
    lo = (x - hi.astype(F32)).astype(BF16)
    return hi, lo


def matmul(a, b):
    return jnp.dot(a, b, preferred_element_type=F32)


def from_left(table, x):
    hi, lo = halves(x)
    return matmul(table, jnp.concatenate([hi, lo, hi], axis=0))


def from_right(x, table):
    hi, lo = halves(x)
    return matmul(jnp.concatenate([hi, lo, hi], axis=1), table)


def tables_kernel(probe_ref, fre, fro, fle, flo, ire, iro, ile, ilo, perm, peak, *, pixels):
    half = pixels // 2
    row = lax.broadcasted_iota(jnp.int32, (half, half), 0)
    col = lax.broadcasted_iota(jnp.int32, (half, half), 1)
    scale = 1.0 / math.sqrt(pixels)

    def waves(n, m, parity):
        turns = (n * (2 * m + parity)) & (pixels - 1)
        turns = jnp.where(turns > half, turns - pixels, turns)
        angle = turns.astype(F32) * (2.0 * math.pi / pixels)
        return jnp.cos(angle) * scale, jnp.sin(angle) * scale

    c_e, s_e = waves(row, col, 0)
    c_o, s_o = waves(row, col, 1)
    c_t, s_t = waves(col, row, 1)

    def square(a, b, c, d):
        return jnp.concatenate(
            [jnp.concatenate([a, b], axis=1), jnp.concatenate([c, d], axis=1)], axis=0
        )

    for w, down, across in (
        (square(c_e, -s_e, s_e, c_e), fre, ile),
        (square(c_o, -s_o, s_o, c_o), fro, ilo),
        (square(c_e, s_e, -s_e, c_e), ire, fle),
        (square(c_t, s_t, -s_t, c_t), iro, flo),
    ):
        hi, lo = halves(w)
        for i, x in enumerate((hi, hi, lo)):
            down[pl.ds(i * pixels, pixels), :] = x
            across[:, pl.ds(i * pixels, pixels)] = x

    x = lax.broadcasted_iota(jnp.int32, (pixels, pixels), 0)
    j = lax.broadcasted_iota(jnp.int32, (pixels, pixels), 1)
    target = jnp.where(j < half, 2 * j, 2 * (j - half) + 1)
    one = jnp.where(x == target, 1.0, 0.0).astype(BF16)
    for i in range(3):
        perm[pl.ds(i * pixels, pixels), :] = one

    total = None
    for part in range(probe_ref.shape[0]):
        for k in range(probe_ref.shape[1]):
            t = probe_ref[part, k]
            total = t * t if total is None else total + t * t
    peak[...] = jnp.broadcast_to(
        jnp.max(jnp.max(total, axis=0, keepdims=True), axis=1, keepdims=True), peak.shape
    )


def fold_block(x):
    rows, cols = x.shape
    y = jnp.sum(x.reshape(rows // SUB, SUB, cols), axis=0)
    z = y[:, :LANE]
    for c in range(LANE, cols, LANE):
        z = z + y[:, c : c + LANE]
    return z


def forward_kernel(
    pos_ref, cnt_ref, *refs, modes, pixels, tile, grid_shape, chunks
):
    n_pieces = 7
    pieces = refs[:n_pieces]
    probe_ref, amp_left, amp_right, fre, fro, fle, flo, perm = refs[n_pieces : n_pieces + 8]
    patch_ref, energy_ref = refs[n_pieces + 8 : n_pieces + 10]
    g_refs = refs[n_pieces + 10 : n_pieces + 10 + len(chunks)]
    ext, far, sem = refs[n_pieces + 10 + len(chunks) :]
    s = pl.program_id(0)
    half = pixels // 2

    @pl.when(s == 0)
    def _():
        copies = []
        for i, (piece, p0, r0, c0, rn, cn) in enumerate(grid_shape):
            copies.append(
                pltpu.make_async_copy(
                    pieces[piece].at[:, pl.ds(p0, rn), :],
                    ext.at[:, pl.ds(r0, rn), pl.ds(c0, cn)],
                    sem.at[i],
                )
            )
        for c in copies:
            c.start()
        energy_ref[...] = jnp.zeros_like(energy_ref)
        for c in copies:
            c.wait()

    @pl.when(s < cnt_ref[0])
    def _():
        a = pos_ref[s, 0]
        b = pos_ref[s, 1]
        qa, qb = a // SUB, b // LANE
        ta, tb = a - qa * SUB, b - qb * LANE
        rows, cols = pixels + SUB, pixels + LANE
        r0 = pl.multiple_of(qa * SUB, SUB)
        c0 = pl.multiple_of(qb * LANE, LANE)
        parts = []
        for part in range(2):
            blk = ext[part, pl.ds(r0, rows), pl.ds(c0, cols)]
            blk = pltpu.roll(blk, lax.rem(cols - tb, cols), 1)[:, :pixels]
            blk = pltpu.roll(blk, lax.rem(rows - ta, rows), 0)[:pixels]
            parts.append(blk)
            patch_ref[0, part] = blk
        energy_ref[...] += fold_block(parts[0] * parts[0] + parts[1] * parts[1])

        total_e = None
        for k in range(modes):
            o_r, o_i = patch_ref[0, 0], patch_ref[0, 1]
            p_r, p_i = probe_ref[0, k], probe_ref[1, k]
            w_r = p_r * o_r - p_i * o_i
            w_i = p_r * o_i + p_i * o_r
            even = jnp.concatenate(
                [w_r[:half] + w_r[half:], w_i[:half] + w_i[half:]], axis=0
            )
            odd = jnp.concatenate(
                [w_r[:half] - w_r[half:], w_i[:half] - w_i[half:]], axis=0
            )
            ue = from_left(fle[...], even)
            uo = from_left(flo[...], odd)
            u_r = jnp.concatenate([ue[:half], uo[:half]], axis=0)
            u_i = jnp.concatenate([ue[half:], uo[half:]], axis=0)
            be = jnp.concatenate(
                [u_r[:, :half] + u_r[:, half:], u_i[:, :half] + u_i[:, half:]], axis=1
            )
            bo = jnp.concatenate(
                [u_r[:, :half] - u_r[:, half:], u_i[:, :half] - u_i[:, half:]], axis=1
            )
            far[k, 0] = from_right(be, fre[...])
            far[k, 1] = from_right(bo, fro[...])

        amp = jnp.concatenate(
            [
                jnp.concatenate([ref[0, pl.ds(p, half, stride=2), :] for p in range(2)], axis=0)
                for ref in (amp_left, amp_right)
            ],
            axis=1,
        )
        a_hi = amp.astype(BF16)
        a_rest = amp - a_hi.astype(F32)
        a_mid, a_lo = halves(a_rest)
        amp = matmul(jnp.concatenate([a_hi, a_mid, a_lo], axis=1), perm[...])
        for p in range(2):
            inten = None
            for k in range(modes):
                f = far[k, p]
                t = f * f
                t = t[:, :half] + t[:, half:]
                inten = t if inten is None else inten + t
            mod = amp[:, p * half : (p + 1) * half] * lax.rsqrt(
                jnp.maximum(inten, INTENSITY_FLOOR)
            )
            mod = jnp.concatenate([mod, mod], axis=1)
            for c, group in enumerate(chunks):
                for i, k in enumerate(group):
                    hi, lo = halves(far[k, p] * mod)
                    g_refs[c][0, i, p, 0] = hi
                    g_refs[c][0, i, p, 1] = lo


def backward_kernel(cnt_ref, *refs, modes, pixels, first):
    if first:
        g_ref, patch_ref, probe_ref, energy_ref, ire, iro, ile, ilo, grad_ref, pgrad_ref = refs
        prev_ref = None
    else:
        (g_ref, patch_ref, probe_ref, energy_ref, ire, iro, ile, ilo, prev_ref,
         grad_ref, pgrad_ref) = refs
    s = pl.program_id(0)
    half = pixels // 2
    share = pgrad_ref.shape[1] - SUB
    per_plane = pixels // share
    live = s < cnt_ref[0]

    @pl.when(s == 0)
    def _():
        pgrad_ref[...] = jnp.zeros_like(pgrad_ref)
        for i in range(pgrad_ref.shape[0]):
            pgrad_ref[i, pl.ds(share, SUB), pl.ds(0, LANE)] = energy_ref[...]

    @pl.when(jnp.logical_not(live))
    def _():
        grad_ref[...] = jnp.zeros_like(grad_ref)

    @pl.when(live)
    def _():
        for i in range(modes):
            e_hi, e_lo = g_ref[0, i, 0, 0], g_ref[0, i, 0, 1]
            o_hi, o_lo = g_ref[0, i, 1, 0], g_ref[0, i, 1, 1]
            e = matmul(jnp.concatenate([e_hi, e_lo, e_hi], axis=1), ire[...])
            o = matmul(jnp.concatenate([o_hi, o_lo, o_hi], axis=1), iro[...])
            x0, x1 = e + o, e - o
            ke = jnp.concatenate(
                [
                    jnp.concatenate([x0[:half, :half], x1[:half, :half]], axis=1),
                    jnp.concatenate([x0[:half, half:], x1[:half, half:]], axis=1),
                ],
                axis=0,
            )
            ko = jnp.concatenate(
                [
                    jnp.concatenate([x0[half:, :half], x1[half:, :half]], axis=1),
                    jnp.concatenate([x0[half:, half:], x1[half:, half:]], axis=1),
                ],
                axis=0,
            )
            ev = from_left(ile[...], ke)
            od = from_left(ilo[...], ko)
            for h in range(2):
                rs = pl.ds(h * half, half)
                back = ev + od if h == 0 else ev - od
                b_r, b_i = back[:half], back[half:]
                o_r, o_i = patch_ref[0, 0, rs, :], patch_ref[0, 1, rs, :]
                p_r, p_i = probe_ref[0, i, rs, :], probe_ref[1, i, rs, :]
                f_r = b_r - (p_r * o_r - p_i * o_i)
                f_i = b_i - (p_r * o_i + p_i * o_r)
                g_r = p_r * f_r + p_i * f_i
                g_i = p_r * f_i - p_i * f_r
                if i == 0 and first:
                    grad_ref[0, 0, rs, :] = g_r
                    grad_ref[0, 1, rs, :] = g_i
                elif i == 0:
                    grad_ref[0, 0, rs, :] = prev_ref[0, 0, rs, :] + g_r
                    grad_ref[0, 1, rs, :] = prev_ref[0, 1, rs, :] + g_i
                else:
                    grad_ref[0, 0, rs, :] += g_r
                    grad_ref[0, 1, rs, :] += g_i
                t_r = o_r * f_r + o_i * f_i
                t_i = o_r * f_i - o_i * f_r
                for q in range(half // share):
                    at = h * (half // share) + q
                    cut = slice(q * share, (q + 1) * share)
                    pgrad_ref[i * per_plane + at, pl.ds(0, share), :] += t_r[cut]
                    pgrad_ref[(modes + i) * per_plane + at, pl.ds(0, share), :] += t_i[cut]


def place_kernel(pos_ref, cnt_ref, grad_ref, *refs, pixels, grid_shape):
    outs = refs[: len(grid_shape)]
    canvas, sem = refs[len(grid_shape) :]
    canvas[...] = jnp.zeros_like(canvas)
    rows, cols = pixels + SUB, pixels + LANE

    def step(s, carry):
        a = pos_ref[s, 0]
        b = pos_ref[s, 1]
        qa, qb = a // SUB, b // LANE
        ta, tb = a - qa * SUB, b - qb * LANE
        r0 = pl.multiple_of(qa * SUB, SUB)
        c0 = pl.multiple_of(qb * LANE, LANE)
        for part in range(2):
            g = grad_ref[s, part]
            g = jnp.concatenate([g, jnp.zeros((SUB, pixels), F32)], axis=0)
            g = pltpu.roll(g, ta, 0)
            g = jnp.concatenate([g, jnp.zeros((rows, LANE), F32)], axis=1)
            g = pltpu.roll(g, tb, 1)
            canvas[part, pl.ds(r0, rows), pl.ds(c0, cols)] += g
        return carry

    lax.fori_loop(0, cnt_ref[0], step, 0)
    copies = []
    for i, (_, _, r0, c0, rn, cn) in enumerate(grid_shape):
        copies.append(
            pltpu.make_async_copy(
                canvas.at[:, pl.ds(r0, rn), pl.ds(c0, cn)], outs[i], sem.at[i]
            )
        )
    for c in copies:
        c.start()
    for c in copies:
        c.wait()


def slope_kernel(pos_ref, cnt_ref, grad_ref, *refs, pixels, grid_shape, extent):
    pieces = refs[:-3]
    out_ref, ext, sem = refs[-3:]
    s = pl.program_id(0)
    out_ref[...] = jnp.zeros_like(out_ref)

    @pl.when(s == 0)
    def _():
        copies = []
        for i, (piece, p0, r0, c0, rn, cn) in enumerate(grid_shape):
            copies.append(
                pltpu.make_async_copy(
                    pieces[piece].at[:, pl.ds(p0, rn), :],
                    ext.at[:, pl.ds(r0, rn), pl.ds(c0, cn)],
                    sem.at[i],
                )
            )
        for c in copies:
            c.start()
        for c in copies:
            c.wait()

    @pl.when(s < cnt_ref[0])
    def _():
        rows, cols = pixels + 2 * SUB, pixels + 2 * LANE
        a = pos_ref[s, 0]
        b = pos_ref[s, 1]
        qa = jnp.minimum((a - 1) // SUB, (extent - rows) // SUB)
        qb = jnp.minimum((b - 1) // LANE, (extent - cols) // LANE)
        ta, tb = a - qa * SUB, b - qb * LANE
        r0 = pl.multiple_of(qa * SUB, SUB)
        c0 = pl.multiple_of(qb * LANE, LANE)
        acc_r = jnp.zeros((SUB, LANE), F32)
        acc_c = jnp.zeros((SUB, LANE), F32)
        for part in range(2):
            w = ext[part, pl.ds(r0, rows), pl.ds(c0, cols)]
            w = pltpu.roll(w, lax.rem(cols + LANE - tb, cols), 1)
            w = pltpu.roll(w, lax.rem(rows + SUB - ta, rows), 0)
            g = grad_ref[0, part]
            mid = w[:, LANE : LANE + pixels]
            down = pltpu.roll(mid, rows - 1, 0)[SUB : SUB + pixels]
            up = pltpu.roll(mid, 1, 0)[SUB : SUB + pixels]
            acc_r = acc_r + fold_block(g * (down - up))
            band = w[SUB : SUB + pixels]
            right = pltpu.roll(band, cols - 1, 1)[:, LANE : LANE + pixels]
            left = pltpu.roll(band, 1, 1)[:, LANE : LANE + pixels]
            acc_c = acc_c + fold_block(g * (right - left))
        out_ref[0, 0] = acc_r
        out_ref[0, 1] = acc_c


def neighbour(x, axis, by):
    peers = lax.axis_size(axis)
    pairs = [(i, i + by) for i in range(peers) if 0 <= i + by < peers]
    return lax.ppermute(x, axis, pairs)


def body(object_field, probe, amplitudes, positions, counts):
    tile = object_field.shape[1]
    modes, pixels = probe.shape[1], probe.shape[2]
    slots = positions.shape[2]
    extent = tile + 2 * HALO
    pos = positions[0, 0]
    cnt = counts[0]
    chunks = tuple(
        tuple(range(i, i + 4)) for i in range(0, modes, 4)
    ) if modes != 4 else CHUNKS

    lo, hi = HALO, HALO + tile
    left = neighbour(object_field[:, :, tile - HALO :], "col", 1)
    right = neighbour(object_field[:, :, :HALO], "col", -1)
    above = neighbour(object_field[:, tile - HALO :, :], "row", 1)
    below = neighbour(object_field[:, :HALO, :], "row", -1)
    both = jnp.concatenate([above, below], axis=1)
    left_ends = neighbour(both[:, :, tile - HALO :], "col", 1)
    right_ends = neighbour(both[:, :, :HALO], "col", -1)
    pieces = [object_field, left, right, above, below, left_ends, right_ends]
    load_map = [
        (0, 0, lo, lo, tile, tile),
        (1, 0, lo, 0, tile, HALO),
        (2, 0, lo, hi, tile, HALO),
        (3, 0, 0, lo, HALO, tile),
        (4, 0, hi, lo, HALO, tile),
        (5, 0, 0, 0, HALO, HALO),
        (5, HALO, hi, 0, HALO, HALO),
        (6, 0, 0, hi, HALO, HALO),
        (6, HALO, hi, hi, HALO, HALO),
    ]
    store_map = [
        (0, 0, lo, lo, tile, tile),
        (1, 0, lo, 0, tile, HALO),
        (2, 0, lo, hi, tile, HALO),
        (3, 0, 0, 0, HALO, extent),
        (4, 0, hi, 0, HALO, extent),
    ]

    any_spec = pl.BlockSpec(memory_space=pl.ANY)
    down = jax.ShapeDtypeStruct((3 * pixels, pixels), BF16)
    across = jax.ShapeDtypeStruct((pixels, 3 * pixels), BF16)
    *made, perm, peak = pl.pallas_call(
        functools.partial(tables_kernel, pixels=pixels),
        out_shape=[down, down, across, across] * 2
        + [down, jax.ShapeDtypeStruct((SUB, LANE), F32)],
        compiler_params=pltpu.CompilerParams(vmem_limit_bytes=40 << 20),
        name="tables",
    )(probe)
    fwd_tables, inv_tables = made[:4], made[4:]
    illumination = peak[0, 0]

    def whole(x):
        nd = x.ndim
        return pl.BlockSpec(x.shape, lambda s, *_: (0,) * nd)

    patch_spec = pl.BlockSpec((1, 2, pixels, pixels), lambda s, *_: (s, 0, 0, 0))
    grad_shape = jax.ShapeDtypeStruct((slots, 2, pixels, pixels), F32)

    def g_spec(group):
        return pl.BlockSpec(
            (1, len(group), 2, 2, pixels, pixels), lambda s, *_: (s, 0, 0, 0, 0, 0)
        )

    outs = pl.pallas_call(
        functools.partial(
            forward_kernel,
            modes=modes,
            pixels=pixels,
            tile=tile,
            grid_shape=load_map,
            chunks=chunks,
        ),
        grid_spec=pltpu.PrefetchScalarGridSpec(
            num_scalar_prefetch=2,
            grid=(slots,),
            in_specs=[any_spec] * len(pieces)
            + [whole(probe)]
            + [
                pl.BlockSpec((1, pixels, pixels // 2), lambda s, *_: (s, 0, 0)),
                pl.BlockSpec((1, pixels, pixels // 2), lambda s, *_: (s, 0, 1)),
            ]
            + [whole(t) for t in fwd_tables]
            + [whole(perm)],
            out_specs=[patch_spec, pl.BlockSpec((SUB, LANE), lambda s, *_: (0, 0))]
            + [g_spec(g) for g in chunks],
            scratch_shapes=[
                pltpu.VMEM((2, extent, extent), F32),
                pltpu.VMEM((modes, 2, pixels, pixels), F32),
                pltpu.SemaphoreType.DMA((len(load_map),)),
            ],
        ),
        out_shape=[grad_shape, jax.ShapeDtypeStruct((SUB, LANE), F32)]
        + [
            jax.ShapeDtypeStruct((slots, len(g), 2, 2, pixels, pixels), BF16) for g in chunks
        ],
        compiler_params=pltpu.CompilerParams(vmem_limit_bytes=56 << 20),
        name="forward",
    )(pos, cnt, *pieces, probe, amplitudes[0, 0], amplitudes[0, 0], *fwd_tables, perm)
    patches, energy_block = outs[0], outs[1]
    gs = outs[2:]

    grad = None
    probe_parts = []
    devices = lax.axis_size("row") * lax.axis_size("col")
    me = lax.axis_index(("row", "col"))
    for group, g in zip(chunks, gs):
        n = len(group)
        part = probe[:, group[0] : group[0] + n] if n != modes else probe
        first = grad is None
        share = 2 * n * pixels // devices
        grad, pgrad = pl.pallas_call(
            functools.partial(backward_kernel, modes=n, pixels=pixels, first=first),
            grid_spec=pltpu.PrefetchScalarGridSpec(
                num_scalar_prefetch=1,
                grid=(slots,),
                in_specs=[g_spec(group), patch_spec, whole(part), whole(energy_block)]
                + [whole(t) for t in inv_tables]
                + ([] if first else [patch_spec]),
                out_specs=[
                    patch_spec,
                    pl.BlockSpec((devices, share + SUB, pixels), lambda s, *_: (0, 0, 0)),
                ],
            ),
            out_shape=[
                grad_shape,
                jax.ShapeDtypeStruct((devices, share + SUB, pixels), F32),
            ],
            compiler_params=pltpu.CompilerParams(vmem_limit_bytes=56 << 20),
            name="backward",
        )(cnt, g, patches, part, energy_block, *inv_tables, *([] if first else [grad]))
        mine = pgrad.reshape(-1, pixels)
        for axis in ("row", "col"):
            mine = lax.psum_scatter(mine, axis, scatter_dimension=0, tiled=True)
        energy = jnp.sum(mine[share:, :LANE]) * (1.0 / (pixels * pixels))
        own = lax.dynamic_slice_in_dim(part.reshape(-1, pixels), me * share, share, 0)
        new = own + mine[:share] / (energy + EPSILON)
        new = lax.all_gather(new, ("row", "col"), axis=0, tiled=True)
        probe_parts.append(new.reshape(2, n, pixels, pixels))
    probe_new = (
        probe_parts[0] if len(probe_parts) == 1 else jnp.concatenate(probe_parts, axis=1)
    )

    placed = pl.pallas_call(
        functools.partial(place_kernel, pixels=pixels, grid_shape=store_map),
        grid_spec=pltpu.PrefetchScalarGridSpec(
            num_scalar_prefetch=2,
            grid=(1,),
            in_specs=[whole(grad)],
            out_specs=[any_spec] * len(store_map),
            scratch_shapes=[
                pltpu.VMEM((2, extent, extent), F32),
                pltpu.SemaphoreType.DMA((len(store_map),)),
            ],
        ),
        out_shape=[jax.ShapeDtypeStruct((2, rn, cn), F32) for *_, rn, cn in store_map],
        compiler_params=pltpu.CompilerParams(vmem_limit_bytes=56 << 20),
        name="place",
    )(pos, cnt, grad)
    centre, to_left, to_right, to_above, to_below = placed
    from_right = neighbour(to_left, "col", -1)
    from_left = neighbour(to_right, "col", 1)
    from_below = neighbour(to_above, "row", -1)
    from_above = neighbour(to_below, "row", 1)
    both = jnp.concatenate([from_above, from_below], axis=1)
    ends_right = neighbour(both[:, :, :HALO], "col", -1)
    ends_left = neighbour(both[:, :, hi:], "col", 1)

    slopes = pl.pallas_call(
        functools.partial(
            slope_kernel, pixels=pixels, grid_shape=load_map, extent=extent
        ),
        grid_spec=pltpu.PrefetchScalarGridSpec(
            num_scalar_prefetch=2,
            grid=(slots,),
            in_specs=[patch_spec] + [any_spec] * len(pieces),
            out_specs=pl.BlockSpec((1, 2, SUB, LANE), lambda s, *_: (s, 0, 0, 0)),
            scratch_shapes=[
                pltpu.VMEM((2, extent, extent), F32),
                pltpu.SemaphoreType.DMA((len(load_map),)),
            ],
        ),
        out_shape=jax.ShapeDtypeStruct((slots, 2, SUB, LANE), F32),
        compiler_params=pltpu.CompilerParams(vmem_limit_bytes=56 << 20),
        name="slopes",
    )(pos, cnt, grad, *pieces)
    position_grad = (jnp.sum(slopes, axis=(2, 3)) * (0.5 / pixels))[None, None]

    wide = tile - HALO

    def lay(x, axis, start):
        pads = [(0, 0)] * 3
        pads[axis] = (start, tile - start - x.shape[axis])
        return jnp.pad(x, pads)

    edge_right = from_right + lay(ends_right[:, :HALO], 1, 0) + lay(ends_right[:, HALO:], 1, wide)
    edge_left = from_left + lay(ends_left[:, :HALO], 1, 0) + lay(ends_left[:, HALO:], 1, wide)
    fold = (
        centre
        + lay(edge_left, 2, 0)
        + lay(edge_right, 2, wide)
        + lay(from_above[:, :, lo:hi], 1, 0)
        + lay(from_below[:, :, lo:hi], 1, wide)
    )
    object_new = object_field + fold / illumination
    return (object_new, probe_new, position_grad)


def solution(mesh):
    return jax.shard_map(
        body,
        mesh=mesh,
        in_specs=(
            P(None, "row", "col"),
            P(),
            P("row", "col", None, None, None),
            P("row", "col", None, None),
            P("row", "col"),
        ),
        out_specs=(P(None, "row", "col"), P(), P("row", "col", None, None)),
        check_vma=False,
    )
```
